32 devices in a mesh: expert: 8 (over z, x), tensor: 4 (over y, core).
Axes of the slice: x: 2, y: 2, z: 4, core: 2. Of those that a mesh axis runs over, the one named last changes fastest.
Arguments:
- tokens: bfloat16 [1024, 4096], P('expert', 'tensor'), may hold values from -6 to 6
- expert_ids: int32 [1024, 8], P('expert'), may hold values from 0 to 15, all different within a row; in each aligned block of 128 rows (0 to 127, 128 to 255, ...) at most 96 rows name the same one
- combine_weight: float32 [1024, 8], P('expert'), may hold values from 0.05 to 0.5
- gate_weight: bfloat16 [16, 4096, 1024], P('expert', 'tensor'), may hold values from -0.09375 to 0.09375
- up_weight: bfloat16 [16, 4096, 1024], P('expert', 'tensor'), may hold values from -0.09375 to 0.09375
- down_weight: bfloat16 [16, 1024, 4096], P('expert', None, 'tensor'), may hold values from -0.1875 to 0.1875
- out_cotangent: bfloat16 [1024, 4096], P('expert', 'tensor'), may hold values from -3 to 3
Outputs:
- mixed: bfloat16 [1024, 4096], P('expert', 'tensor')
- token_grad: bfloat16 [1024, 4096], P('expert', 'tensor')
- combine_grad: float32 [1024, 8], P('expert')
- gate_grad: bfloat16 [16, 4096, 1024], P('expert', 'tensor')
- up_grad: bfloat16 [16, 4096, 1024], P('expert', 'tensor')
- down_grad: bfloat16 [16, 1024, 4096], P('expert', None, 'tensor')
The draws below stay inside these ranges and needn't reach their ends.
Inputs may be any that keep to these rules, and one draw needn't show every extreme that they name: `expert_ids`: each row names 8 different experts. Among the rows of one device no expert is named by more than 96 rows, a bound that some block reaches.
All inputs are finite; a program needn't handle non-finite values.
Results may differ from the reference program's by a relative error of at most 0.023.
Values may be sent and summed in bfloat16 or wider, within the bound.
A program may use at most 128 MiB of HBM per device.

```python
import math
import jax
import jax.numpy as jnp
import numpy as np
from jax import lax

D = 4096
EXPERT_HIDDEN = 1024
TOP = 8
TOK_DEV = 128
EXPERTS = 16
TOKENS = 1024
CAP = 96
N_EXPERT = 8
N_TENSOR = 4


def levels(own_key, extent, split, low, top_value):
    def one(axis_at, parts):
        steps = jax.random.uniform(jax.random.fold_in(jax.random.fold_in(own_key, 6), axis_at), (parts,), jnp.float32, low / len(split), top_value / len(split))
        return jnp.repeat(jnp.exp(steps), extent[axis_at] // parts).reshape((-1,) + (1,) * (len(extent) - axis_at - 1))

    factor_of = one(*split[0])
    for cut in split[1:]:
        factor_of = factor_of * one(*cut)
    return factor_of


def routed_block(stream_key, own, number, rows, number_of, top, most, slope):
    order = jax.random.permutation(stream_key, number_of)
    packed, common = shares(number_of, rows * top, most, slope, True), shares(number_of, rows * top, most, slope, False)
    places = jnp.arange(number_of)

    def named(lengths, rotation):
        used = int((lengths > 0).sum())
        fixed = max(1, used // 4)
        shifted = fixed + (places - fixed + rotation * (used - fixed)) % max(1, number_of - fixed)
        return jnp.zeros((number_of,), jnp.int32).at[order[jnp.where(places < fixed, places, shifted)]].set(jnp.asarray(lengths, jnp.int32))

    lengths = jnp.where(number % 4 == 0, named(packed, number // 4), named(common, number - number // 4 - 1))
    mixed = jax.random.permutation(jax.random.fold_in(own, 3), number_of)
    source_of, receiver = mixed[0:number_of // 2 * 2:2], mixed[1:number_of // 2 * 2:2]
    margin = jnp.minimum(lengths[source_of] - 1, most - lengths[receiver]) // 2
    margin = jnp.where((source_of == order[0]) | (receiver == order[0]) | (lengths[receiver] == 0), 0, jnp.maximum(margin, 0))
    shifted = jax.random.randint(jax.random.fold_in(own, 4), (number_of // 2,), 0, 1 << 20) % (margin + 1)
    lengths = lengths.at[source_of].add(-shifted).at[receiver].add(shifted)
    labels = jnp.searchsorted(jnp.cumsum(lengths), jnp.arange(rows * top), side="right").astype(jnp.int32)
    table = labels.reshape(top, rows).T
    table = table[jax.random.permutation(jax.random.fold_in(own, 1), rows)]
    rotation = jax.random.randint(jax.random.fold_in(own, 2), (rows, 1), 0, top)
    return jnp.take_along_axis(table, (jnp.arange(top)[None, :] + rotation) % top, axis=1)


def shares(count, total, bound, slope, full):
    weights = [(1 << 20) // math.isqrt(rank ** slope) + 1 for rank in range(1, count + 1)]
    largest = bound if full else min(bound, max(-(-total // count), total * weights[0] // sum(weights)))
    least = 1 if total - largest >= count - 1 else 0
    given, spare = [largest] + [least] * (count - 1), total - largest - least * (count - 1)
    while spare > 0:
        candidates = [i for i in range(1, count) if given[i] < largest] or [i for i in range(1, count) if given[i] < bound]
        whole, budget = sum([weights[i] for i in candidates]), spare
        for i in candidates:
            extra = min(bound - given[i], max(1, budget * weights[i] // whole), spare)
            given[i] = given[i] + extra
            spare = spare - extra
    return np.array(given)


def centred(key, dims, spread, reach, shards=(), kind=jnp.bfloat16):
    result = jax.random.normal(key, dims, jnp.float32) * spread
    if len(shards) > 0:
        result = levels(key, dims, shards, -0.22, 0.18) * result
    return jnp.clip(result, min=-reach, max=reach).astype(kind)


def setup_inputs(seed: int = 0) -> dict:
    arg_keys = jax.random.split(jax.random.key(seed), 8)
    tokens = centred(arg_keys[0], (TOKENS, D), 1.0, 6.0, ((0, 8), (1, 4)))
    expert_ids_keys = jax.random.split(jax.random.fold_in(arg_keys[1], 1), TOKENS // TOK_DEV)
    expert_ids_turns = jax.random.permutation(jax.random.fold_in(arg_keys[1], 3), TOKENS // TOK_DEV)
    expert_ids = jax.vmap(lambda own, number: routed_block(jax.random.fold_in(arg_keys[1], 2), own, number, TOK_DEV, EXPERTS, TOP, CAP, 2))(expert_ids_keys, expert_ids_turns).reshape((TOKENS, TOP))
    combine_weight = jnp.clip(jnp.exp(math.log(0.5) - 2.3025851 * jax.random.uniform(arg_keys[2], (TOKENS, TOP), jnp.float32) ** levels(arg_keys[2], (TOKENS, TOP), ((0, 8),), -0.2, 0.2)), 0.05, 0.5)
    gate_weight = centred(arg_keys[3], (EXPERTS, D, EXPERT_HIDDEN), D ** -0.5, 0.09375, ((0, 8), (1, 4)))
    up_weight = centred(arg_keys[4], (EXPERTS, D, EXPERT_HIDDEN), D ** -0.5, 0.09375, ((0, 8), (1, 4)))
    down_weight = centred(arg_keys[5], (EXPERTS, EXPERT_HIDDEN, D), EXPERT_HIDDEN ** -0.5, 0.1875, ((0, 8), (2, 4)))
    out_cotangent = centred(arg_keys[6], (TOKENS, D), 0.5, 3.0, ((0, 8), (1, 4)))
    return {"tokens": tokens, "expert_ids": expert_ids, "combine_weight": combine_weight, "gate_weight": gate_weight, "up_weight": up_weight, "down_weight": down_weight, "out_cotangent": out_cotangent}


def rounded(value):
    return lax.optimization_barrier(value.astype(jnp.bfloat16)).astype(jnp.float32)


def block_total_sum(left, right_blocks, form):
    return jnp.sum(rounded(jnp.einsum(form, left, right_blocks, precision=lax.Precision.HIGHEST)), axis=0)


def reference(tokens, expert_ids, combine_weight, gate_weight, up_weight, down_weight, out_cotangent):
    pair_block = TOK_DEV * TOP
    pair_total = TOKENS * TOP
    capacity_slot_rows = N_EXPERT * CAP
    partial_share = D // N_TENSOR
    block_ids = expert_ids.reshape(N_EXPERT, pair_block)
    onehot = (block_ids[:, :, None] == jnp.arange(EXPERTS, dtype=jnp.int32)[None, None, :]).astype(jnp.int32)
    position = jnp.sum(jnp.cumsum(onehot, axis=1) * onehot, axis=2) - 1
    row_within = jnp.arange(N_EXPERT, dtype=jnp.int32)[:, None] * CAP + position
    pair_index = jnp.arange(pair_total, dtype=jnp.int32)
    table = jnp.full((EXPERTS, capacity_slot_rows), pair_total, jnp.int32)
    table = table.at[expert_ids.reshape(pair_total), row_within.reshape(pair_total).astype(jnp.int32)].set(pair_index)
    flat_weight = combine_weight.reshape(pair_total).astype(jnp.float32)
    cotangent = out_cotangent.astype(jnp.float32)
    highest = lax.Precision.HIGHEST

    def per_expert(carry, inputs):
        mixed_acc, grad_acc, combine_acc = carry
        rows, gate_w, up_w, down_w = inputs
        filled = rows < pair_total
        safe = jnp.minimum(rows, pair_total - 1)
        token_of = safe // TOP
        weight = jnp.where(filled, flat_weight[safe], jnp.float32(0.0))
        routed = jnp.where(filled[:, None], tokens[token_of].astype(jnp.float32), jnp.float32(0.0))
        incoming_gradient = rounded(weight[:, None] * cotangent[token_of])
        gate_matrix_float = gate_w.astype(jnp.float32)
        up_matrix_float = up_w.astype(jnp.float32)
        down_matrix_float = down_w.astype(jnp.float32)
        dispatched_blocks = routed.reshape(capacity_slot_rows, N_TENSOR, partial_share)
        gate_matrix = block_total_sum(dispatched_blocks, gate_matrix_float.reshape(N_TENSOR, partial_share, EXPERT_HIDDEN), "oem,eml->eol")
        up_matrix = block_total_sum(dispatched_blocks, up_matrix_float.reshape(N_TENSOR, partial_share, EXPERT_HIDDEN), "oem,eml->eol")
        hidden_act = rounded(jax.nn.silu(gate_matrix) * up_matrix)
        expert_out = rounded(jnp.dot(hidden_act, down_matrix_float, precision=highest))
        hidden_state_cotangent = block_total_sum(incoming_gradient.reshape(capacity_slot_rows, N_TENSOR, partial_share), down_matrix_float.reshape(EXPERT_HIDDEN, N_TENSOR, partial_share), "elb,glb->leg")
        down_grad = jnp.dot(hidden_act.T, incoming_gradient, precision=highest).astype(jnp.bfloat16)
        sigma = jax.nn.sigmoid(gate_matrix)
        gate_diff = rounded(hidden_state_cotangent * up_matrix * sigma * (1.0 + gate_matrix * (1.0 - sigma)))
        up_diff = rounded(hidden_state_cotangent * jax.nn.silu(gate_matrix))
        routed_grad = rounded(jnp.dot(gate_diff, gate_matrix_float.T, precision=highest) + jnp.dot(up_diff, up_matrix_float.T, precision=highest))
        gate_grad = jnp.dot(routed.T, gate_diff, precision=highest).astype(jnp.bfloat16)
        up_grad = jnp.dot(routed.T, up_diff, precision=highest).astype(jnp.bfloat16)
        mixed_acc = mixed_acc.at[token_of].add(weight[:, None] * expert_out)
        grad_acc = grad_acc.at[token_of].add(routed_grad)
        pair_dot = jnp.where(filled, jnp.sum(cotangent[token_of] * expert_out, axis=1), jnp.float32(0.0))
        combine_acc = combine_acc.at[safe].add(pair_dot)
        return (mixed_acc, grad_acc, combine_acc), (gate_grad, up_grad, down_grad)

    start_carry = (jnp.zeros((TOKENS, D), jnp.float32), jnp.zeros((TOKENS, D), jnp.float32), jnp.zeros((pair_total,), jnp.float32))
    final, grads = lax.scan(per_expert, start_carry, (table, gate_weight, up_weight, down_weight))
    mixed_acc, grad_acc, combine_acc = final
    gate_grads, up_grads, down_grads = grads
    return (mixed_acc.astype(jnp.bfloat16), grad_acc.astype(jnp.bfloat16), combine_acc.reshape(TOKENS, TOP), gate_grads, up_grads, down_grads)
```

```python
import jax
import jax.numpy as jnp
from jax import lax
from jax.sharding import PartitionSpec as P

F32, BF16 = jnp.float32, jnp.bfloat16


def dot(form, left, right):
    return jnp.einsum(form, left, right, preferred_element_type=F32)


def per_device(
    tokens, expert_ids, combine_weight, gate_weight, up_weight, down_weight, out_cotangent
):
    groups = lax.axis_size("expert")
    shards = lax.axis_size("tensor")
    local = gate_weight.shape[0]
    width = tokens.shape[1]
    hidden = gate_weight.shape[2]
    rows = tokens.shape[0]
    top = expert_ids.shape[1]
    experts = local * groups
    capacity = 3 * rows * top // (2 * experts)
    slots = groups * capacity
    total = local * slots
    own = total // shards
    mine = lax.axis_index("expert")

    named = expert_ids[:, :, None] == jnp.arange(experts, dtype=jnp.int32)
    dense_weight = jnp.sum(jnp.where(named, combine_weight[:, :, None], 0.0), axis=1)
    weights_all = lax.all_gather(dense_weight, "expert", axis=0)
    tokens_all = lax.all_gather(tokens, "expert", axis=0)
    cotangent_all = lax.all_gather(out_cotangent, "expert", axis=0)
    weight_tok = lax.dynamic_slice_in_dim(weights_all, mine * local, local, 2)
    weight_tok = weight_tok.transpose(2, 0, 1)
    served = weight_tok > 0.0
    earlier = (jnp.arange(rows)[:, None] < jnp.arange(rows)[None, :]).astype(BF16)
    position = dot("ebs,st->ebt", served.astype(BF16), earlier)
    at_slot = jnp.where(served, position, -1.0).astype(jnp.int32)
    chosen = at_slot[:, :, None, :] == jnp.arange(capacity, dtype=jnp.int32)[:, None]
    place = chosen.astype(BF16)
    weight_slot = jnp.sum(jnp.where(chosen, weight_tok[:, :, None, :], 0.0), axis=3)
    weight_slot = weight_slot.reshape(total, 1)
    weight_own = lax.dynamic_slice_in_dim(
        weight_slot, lax.axis_index("tensor") * own, own, 0
    )

    def dispatch(values):
        return [
            dot("bct,btd->bcd", place[e], values).astype(BF16).reshape(slots, width)
            for e in range(local)
        ]

    def scatter_rows(parts):
        return lax.psum_scatter(
            jnp.concatenate(parts, axis=0), "tensor", scatter_dimension=0, tiled=True
        ).astype(F32)

    def gather_rows(value):
        full = lax.all_gather(value.astype(BF16), "tensor", axis=0, tiled=True)
        return full.reshape(local, slots, hidden)

    def combine(parts):
        total_sum = sum(
            dot("bct,bcd->btd", place[e], parts[e].reshape(groups, capacity, width))
            for e in range(local)
        )
        return lax.psum_scatter(
            total_sum.astype(BF16), "expert", scatter_dimension=0, tiled=True
        ).reshape(rows, width)

    routed = dispatch(tokens_all)
    gate = scatter_rows(
        [dot("cd,dk->ck", routed[e], gate_weight[e]).astype(BF16) for e in range(local)]
    )
    up = scatter_rows(
        [dot("cd,dk->ck", routed[e], up_weight[e]).astype(BF16) for e in range(local)]
    )
    incoming = dispatch(cotangent_all)
    pulled = scatter_rows(
        [dot("cd,kd->ck", incoming[e], down_weight[e]).astype(BF16) for e in range(local)]
    )
    sigma = jax.nn.sigmoid(gate)
    silu = gate * sigma
    act = silu * up
    weighted_act = gather_rows(weight_own * act)
    weighted_pull = weight_own * pulled
    gate_diff = gather_rows(weighted_pull * up * sigma * (1.0 + gate * (1.0 - sigma)))
    up_diff = gather_rows(weighted_pull * silu)

    pair_own = jnp.sum(act * pulled, axis=1)
    pair_all = lax.all_gather(pair_own, "tensor", axis=0, tiled=True)
    pair_all = pair_all.reshape(local, groups, capacity)
    pair_tok = jnp.sum(jnp.where(chosen, pair_all[:, :, :, None], 0.0), axis=2)
    pair_tok = lax.all_to_all(
        pair_tok.transpose(1, 0, 2), "expert", split_axis=0, concat_axis=0, tiled=True
    ).reshape(experts, rows)
    combine_grad = jnp.sum(jnp.where(named, pair_tok.T[:, None, :], 0.0), axis=2)

    mixed = combine(
        [
            dot("ck,kd->cd", weighted_act[e], down_weight[e]).astype(BF16)
            for e in range(local)
        ]
    )
    token_grad = combine(
        [
            (
                dot("ck,dk->cd", gate_diff[e], gate_weight[e])
                + dot("ck,dk->cd", up_diff[e], up_weight[e])
            ).astype(BF16)
            for e in range(local)
        ]
    )
    down_grad = jnp.stack(
        [dot("ck,cd->kd", weighted_act[e], incoming[e]).astype(BF16) for e in range(local)]
    )
    gate_grad = jnp.stack(
        [dot("cd,ck->dk", routed[e], gate_diff[e]).astype(BF16) for e in range(local)]
    )
    up_grad = jnp.stack(
        [dot("cd,ck->dk", routed[e], up_diff[e]).astype(BF16) for e in range(local)]
    )
    return (mixed, token_grad, combine_grad, gate_grad, up_grad, down_grad)


def solution(mesh):
    wide, narrow = P("expert", "tensor"), P("expert", None)
    deep, flat = P("expert", "tensor", None), P("expert", None, "tensor")
    return jax.shard_map(
        per_device,
        mesh=mesh,
        in_specs=(wide, narrow, narrow, deep, deep, flat, wide),
        out_specs=(wide, wide, narrow, deep, deep, flat),
        check_vma=False,
    )
```

```python
import jax
import jax.numpy as jnp
from jax import lax
from jax.experimental import pallas as pl
from jax.experimental.pallas import tpu as pltpu
from jax.sharding import PartitionSpec as P

F32, BF16 = jnp.float32, jnp.bfloat16
MESH = pl.DeviceIdType.MESH
AXES = ("expert", "tensor")


def split_of(axis, size):
    inner = 2 if axis == "tensor" else 1 << ((size.bit_length() - 1) // 2)
    return size // inner, inner


class Job:
    def __init__(self, kind, axis, size, array):
        self.kind, self.axis, self.array = kind, axis, array
        self.outer, self.inner = split_of(axis, size)
        block = array.shape if kind == "gather" else array.shape[1:]
        self.rows = block[0]
        shape = (size,) + block if kind == "gather" else block
        self.out = jax.ShapeDtypeStruct(shape, array.dtype)
        dma = pltpu.SemaphoreType.DMA
        self.scratch = [
            dma((self.outer,)),
            dma((self.outer,)),
            dma((self.outer, self.inner)),
            dma((self.outer, self.inner)),
        ]
        if kind == "gather":
            self.scratch.append(dma(()))
        else:
            self.scratch += [
                pltpu.VMEM((self.outer, self.inner - 1) + block, array.dtype),
                pltpu.VMEM((self.outer - 1,) + block, array.dtype),
                pltpu.VMEM((self.outer - 1,) + block, array.dtype),
            ]

    def bind(self, source, result, scratch):
        self.source, self.result = source, result
        self.out_send, self.out_recv, self.in_send, self.in_recv = scratch[:4]
        self.extra = scratch[4:]
        at = lax.axis_index(self.axis)
        self.hi, self.lo = at // self.inner, at % self.inner
        self.started = []

    def index(self, k, j):
        return lax.rem(self.hi + k, self.outer) * self.inner + lax.rem(self.lo + j, self.inner)

    def device(self, k, j):
        where = self.index(k, j)
        return tuple(where if a == self.axis else lax.axis_index(a) for a in AXES)

    def peers(self):
        return [self.device(k, 0) for k in range(1, self.outer)] + [
            self.device(0, j) for j in range(1, self.inner)
        ]

    def send(self, src, dst, send_sem, recv_sem, k, j):
        copy = pltpu.make_async_remote_copy(
            src_ref=src,
            dst_ref=dst,
            send_sem=send_sem,
            recv_sem=recv_sem,
            device_id=self.device(k, j),
            device_id_type=MESH,
        )
        copy.start()
        self.started.append(copy)

    def arrived(self, dst, send_sem, recv_sem, k, j):
        pltpu.make_async_remote_copy(
            src_ref=dst,
            dst_ref=dst,
            send_sem=send_sem,
            recv_sem=recv_sem,
            device_id=self.device(k, j),
            device_id_type=MESH,
        ).wait_recv()

    def add(self, parts, target):
        step = min(32, self.rows)

        def body(i, carry):
            rows = pl.ds(pl.multiple_of(i * step, step), step)
            total = parts[0][rows, :].astype(F32)
            for part in parts[1:]:
                total = total + part[rows, :].astype(F32)
            target[rows, :] = total.astype(target.dtype)
            return carry

        lax.fori_loop(0, self.rows // step, body, 0)

    def start(self):
        if self.kind == "gather":
            mine = self.result.at[self.index(0, 0)]
            self.own = pltpu.make_async_copy(self.source, mine, self.extra[0])
            self.own.start()
            for k in range(1, self.outer):
                self.send(self.source, mine, self.out_send.at[k], self.out_recv.at[k], k, 0)
            for j in range(1, self.inner):
                self.send(
                    self.source, mine, self.in_send.at[0, j], self.in_recv.at[0, j], 0, j
                )
        else:
            for k in list(range(1, self.outer)) + [0]:
                for j in range(1, self.inner):
                    self.send(
                        self.source.at[self.index(k, j)],
                        self.extra[0].at[k, j - 1],
                        self.in_send.at[k, j],
                        self.in_recv.at[k, j],
                        0,
                        j,
                    )

    def inner_parts(self, k):
        for j in range(1, self.inner):
            self.arrived(
                self.extra[0].at[k, j - 1],
                self.in_send.at[k, j],
                self.in_recv.at[k, j],
                0,
                self.inner - j,
            )
        return [self.source.at[self.index(k, 0)]] + [
            self.extra[0].at[k, j - 1] for j in range(1, self.inner)
        ]

    def relay(self, k):
        if self.kind == "gather":
            slot = self.result.at[self.index(self.outer - k, 0)]
            self.arrived(
                slot, self.out_send.at[k], self.out_recv.at[k], self.outer - k, 0
            )
            for j in range(1, self.inner):
                self.send(slot, slot, self.in_send.at[k, j], self.in_recv.at[k, j], 0, j)
        else:
            staged = self.extra[1].at[k - 1]
            self.add(self.inner_parts(k), staged)
            self.send(
                staged,
                self.extra[2].at[k - 1],
                self.out_send.at[k],
                self.out_recv.at[k],
                k,
                0,
            )

    def finish(self):
        if self.kind == "gather":
            for k in range(self.outer):
                for j in range(1, self.inner):
                    self.arrived(
                        self.result.at[self.index(self.outer - k, self.inner - j)],
                        self.in_send.at[k, j],
                        self.in_recv.at[k, j],
                        0,
                        self.inner - j,
                    )
            self.own.wait()
        else:
            parts = self.inner_parts(0)
            for k in range(1, self.outer):
                slot = self.extra[2].at[k - 1]
                self.arrived(
                    slot, self.out_send.at[k], self.out_recv.at[k], self.outer - k, 0
                )
                parts.append(slot)
            self.add(parts, self.result)
        for copy in self.started:
            copy.wait_send()


def exchange(number, *jobs):
    count = len(jobs)

    def kernel(*refs):
        spare = list(refs[2 * count :])
        for i, job in enumerate(jobs):
            need = len(job.scratch)
            job.bind(refs[i], refs[count + i], spare[:need])
            spare = spare[need:]
        greeted = {job.axis: job for job in jobs}
        barrier = pltpu.get_barrier_semaphore()
        others = [peer for job in greeted.values() for peer in job.peers()]
        for peer in others:
            pl.semaphore_signal(barrier, inc=1, device_id=peer, device_id_type=MESH)
        pl.semaphore_wait(barrier, len(others))
        for job in jobs:
            job.start()
        for k in range(1, max(job.outer for job in jobs)):
            for job in jobs:
                if k < job.outer:
                    job.relay(k)
        for job in jobs:
            job.finish()

    vmem = pl.BlockSpec(memory_space=pltpu.VMEM)
    return pl.pallas_call(
        kernel,
        out_shape=tuple(job.out for job in jobs),
        in_specs=[vmem] * count,
        out_specs=(vmem,) * count,
        scratch_shapes=[item for job in jobs for item in job.scratch],
        compiler_params=pltpu.CompilerParams(collective_id=number, has_side_effects=True),
        name="exchange" + str(number),
    )(*[job.array for job in jobs])


def dot(form, left, right):
    return jnp.einsum(form, left, right, preferred_element_type=F32)


def per_device(
    tokens, expert_ids, combine_weight, gate_weight, up_weight, down_weight, out_cotangent
):
    groups = lax.axis_size("expert")
    shards = lax.axis_size("tensor")
    local = gate_weight.shape[0]
    width = tokens.shape[1]
    hidden = gate_weight.shape[2]
    rows = tokens.shape[0]
    top = expert_ids.shape[1]
    experts = local * groups
    capacity = 3 * rows * top // (2 * experts)
    slots = groups * capacity
    total = local * slots
    own = total // shards
    mine = lax.axis_index("expert")

    named = expert_ids[:, :, None] == jnp.arange(experts, dtype=jnp.int32)
    dense_weight = jnp.sum(jnp.where(named, combine_weight[:, :, None], 0.0), axis=1).T

    def gather(axis, array):
        return Job("gather", axis, lax.axis_size(axis), array)

    def reduce(axis, array):
        return Job("reduce", axis, lax.axis_size(axis), array)

    weights_all, tokens_all = exchange(0, gather("expert", dense_weight), gather("expert", tokens))
    weight_tok = lax.dynamic_slice_in_dim(weights_all, mine * local, local, 1)
    weight_tok = weight_tok.transpose(1, 0, 2)
    served = weight_tok > 0.0
    earlier = (jnp.arange(rows)[:, None] < jnp.arange(rows)[None, :]).astype(BF16)
    position = dot("ebs,st->ebt", served.astype(BF16), earlier)
    at_slot = jnp.where(served, position, -1.0).astype(jnp.int32)
    chosen = at_slot[:, :, None, :] == jnp.arange(capacity, dtype=jnp.int32)[:, None]
    place = chosen.astype(BF16)
    weight_slot = jnp.sum(jnp.where(chosen, weight_tok[:, :, None, :], 0.0), axis=3)
    weight_slot = weight_slot.reshape(total, 1)
    weight_own = lax.dynamic_slice_in_dim(
        weight_slot, lax.axis_index("tensor") * own, own, 0
    )

    def dispatch(values):
        return [
            dot("bct,btd->bcd", place[e], values).astype(BF16).reshape(slots, width)
            for e in range(local)
        ]

    def by_rows(parts):
        return reduce("tensor", jnp.concatenate(parts, axis=0).reshape(shards, own, hidden))

    def rows_of(value):
        return value.reshape(local, slots, hidden)

    def combine(parts):
        total_sum = sum(
            dot("bct,bcd->btd", place[e], parts[e].reshape(groups, capacity, width))
            for e in range(local)
        )
        return reduce("expert", total_sum.astype(BF16))

    routed = dispatch(tokens_all)
    gate_job = by_rows(
        [dot("cd,dk->ck", routed[e], gate_weight[e]).astype(BF16) for e in range(local)]
    )
    up_job = by_rows(
        [dot("cd,dk->ck", routed[e], up_weight[e]).astype(BF16) for e in range(local)]
    )
    gate, up, cotangent_all = exchange(
        1, gate_job, up_job, gather("expert", out_cotangent)
    )
    gate, up = gate.astype(F32), up.astype(F32)
    sigma = jax.nn.sigmoid(gate)
    silu = gate * sigma
    act = silu * up
    incoming = dispatch(cotangent_all)
    pulled_job = by_rows(
        [dot("cd,kd->ck", incoming[e], down_weight[e]).astype(BF16) for e in range(local)]
    )
    pulled, weighted_act = exchange(
        2, pulled_job, gather("tensor", (weight_own * act).astype(BF16))
    )
    pulled, weighted_act = pulled.astype(F32), rows_of(weighted_act)
    weighted_pull = weight_own * pulled
    gate_diff = weighted_pull * up * sigma * (1.0 + gate * (1.0 - sigma))
    up_diff = weighted_pull * silu
    pair_own = jnp.sum(act * pulled, axis=1)
    mixed_job = combine(
        [
            dot("ck,kd->cd", weighted_act[e], down_weight[e]).astype(BF16)
            for e in range(local)
        ]
    )
    mixed, gate_diff, up_diff, pair_all = exchange(
        3,
        mixed_job,
        gather("tensor", gate_diff.astype(BF16)),
        gather("tensor", up_diff.astype(BF16)),
        gather("tensor", pair_own.reshape(1, own)),
    )
    gate_diff, up_diff = rows_of(gate_diff), rows_of(up_diff)
    pair_all = pair_all.reshape(local, groups, capacity)
    pair_tok = jnp.sum(jnp.where(chosen, pair_all[:, :, :, None], 0.0), axis=2)
    pair_wide = lax.dynamic_update_slice_in_dim(
        jnp.zeros((groups, experts, rows), F32), pair_tok.transpose(1, 0, 2), mine * local, 1
    )
    token_job = combine(
        [
            (
                dot("ck,dk->cd", gate_diff[e], gate_weight[e])
                + dot("ck,dk->cd", up_diff[e], up_weight[e])
            ).astype(BF16)
            for e in range(local)
        ]
    )
    token_grad, pair_mine = exchange(4, token_job, reduce("expert", pair_wide))
    combine_grad = jnp.sum(jnp.where(named, pair_mine.T[:, None, :], 0.0), axis=2)
    down_grad = jnp.stack(
        [dot("ck,cd->kd", weighted_act[e], incoming[e]).astype(BF16) for e in range(local)]
    )
    gate_grad = jnp.stack(
        [dot("cd,ck->dk", routed[e], gate_diff[e]).astype(BF16) for e in range(local)]
    )
    up_grad = jnp.stack(
        [dot("cd,ck->dk", routed[e], up_diff[e]).astype(BF16) for e in range(local)]
    )
    return (mixed, token_grad, combine_grad, gate_grad, up_grad, down_grad)


def solution(mesh):
    wide, narrow = P("expert", "tensor"), P("expert", None)
    deep, flat = P("expert", "tensor", None), P("expert", None, "tensor")
    return jax.shard_map(
        per_device,
        mesh=mesh,
        in_specs=(wide, narrow, narrow, deep, deep, flat, wide),
        out_specs=(wide, wide, narrow, deep, deep, flat),
        check_vma=False,
    )
```

```python
import math

import jax
import jax.numpy as jnp
from jax import lax
from jax.experimental import pallas as pl
from jax.experimental.pallas import tpu as pltpu
from jax.sharding import PartitionSpec as P

F32, BF16 = jnp.float32, jnp.bfloat16
MESH = pl.DeviceIdType.MESH
AXES = ("expert", "tensor")


def split_of(axis, size):
    inner = 2 if axis == "tensor" else 1 << ((size.bit_length() - 1) // 2)
    return size // inner, inner


class Job:
    def __init__(self, kind, axis, size, array, chunks=1):
        self.kind, self.axis, self.array = kind, axis, array
        self.outer, self.inner = split_of(axis, size)
        block = array.shape if kind == "gather" else array.shape[1:]
        self.chunks = chunks
        self.rows = block[0] // chunks
        shape = (size,) + block if kind == "gather" else block
        self.out = jax.ShapeDtypeStruct(shape, array.dtype)
        dma = pltpu.SemaphoreType.DMA
        self.scratch = [
            dma((chunks, self.outer)),
            dma((chunks, self.outer)),
            dma((chunks, self.outer, self.inner)),
            dma((chunks, self.outer, self.inner)),
        ]
        if kind == "gather":
            self.scratch.append(dma(()))
        else:
            self.scratch += [
                pltpu.VMEM((self.outer, self.inner - 1) + block, array.dtype),
                pltpu.VMEM((self.outer - 1,) + block, array.dtype),
                pltpu.VMEM((self.outer - 1,) + block, array.dtype),
            ]

    def bind(self, source, result, scratch):
        self.source, self.result = source, result
        self.out_send, self.out_recv, self.in_send, self.in_recv = scratch[:4]
        self.extra = scratch[4:]
        at = lax.axis_index(self.axis)
        self.hi, self.lo = at // self.inner, at % self.inner
        self.started = []

    def index(self, k, j):
        return lax.rem(self.hi + k, self.outer) * self.inner + lax.rem(self.lo + j, self.inner)

    def device(self, k, j):
        where = self.index(k, j)
        return tuple(where if a == self.axis else lax.axis_index(a) for a in AXES)

    def peers(self):
        return [self.device(k, 0) for k in range(1, self.outer)] + [
            self.device(0, j) for j in range(1, self.inner)
        ]

    def send(self, src, dst, send_sem, recv_sem, k, j):
        copy = pltpu.make_async_remote_copy(
            src_ref=src,
            dst_ref=dst,
            send_sem=send_sem,
            recv_sem=recv_sem,
            device_id=self.device(k, j),
            device_id_type=MESH,
        )
        copy.start()
        self.started.append(copy)

    def arrived(self, dst, send_sem, recv_sem, k, j):
        pltpu.make_async_remote_copy(
            src_ref=dst,
            dst_ref=dst,
            send_sem=send_sem,
            recv_sem=recv_sem,
            device_id=self.device(k, j),
            device_id_type=MESH,
        ).wait_recv()

    def add(self, parts, target):
        step = math.gcd(32, self.rows)

        def body(i, carry):
            rows = pl.ds(pl.multiple_of(i * step, step), step)
            total = parts[0][rows, :].astype(F32)
            for part in parts[1:]:
                total = total + part[rows, :].astype(F32)
            target[rows, :] = total.astype(target.dtype)
            return carry

        lax.fori_loop(0, self.rows // step, body, 0)

    def piece(self, c):
        return pl.ds(c * self.rows, self.rows)

    def start(self, c):
        rows = self.piece(c)
        if self.kind == "gather":
            if c == 0:
                mine = self.result.at[self.index(0, 0)]
                self.own = pltpu.make_async_copy(self.source, mine, self.extra[0])
                self.own.start()
            src, dst = self.source.at[rows], self.result.at[self.index(0, 0), rows]
            for k in range(1, self.outer):
                self.send(src, dst, self.out_send.at[c, k], self.out_recv.at[c, k], k, 0)
            for j in range(1, self.inner):
                self.send(
                    src, dst, self.in_send.at[c, 0, j], self.in_recv.at[c, 0, j], 0, j
                )
        else:
            for k in list(range(1, self.outer)) + [0]:
                for j in range(1, self.inner):
                    self.send(
                        self.source.at[self.index(k, j), rows],
                        self.extra[0].at[k, j - 1, rows],
                        self.in_send.at[c, k, j],
                        self.in_recv.at[c, k, j],
                        0,
                        j,
                    )

    def inner_parts(self, c, k):
        rows = self.piece(c)
        for j in range(1, self.inner):
            self.arrived(
                self.extra[0].at[k, j - 1, rows],
                self.in_send.at[c, k, j],
                self.in_recv.at[c, k, j],
                0,
                self.inner - j,
            )
        return [self.source.at[self.index(k, 0), rows]] + [
            self.extra[0].at[k, j - 1, rows] for j in range(1, self.inner)
        ]

    def relay(self, c, k):
        rows = self.piece(c)
        send_sem, recv_sem = self.out_send.at[c, k], self.out_recv.at[c, k]
        if self.kind == "gather":
            slot = self.result.at[self.index(self.outer - k, 0), rows]
            self.arrived(slot, send_sem, recv_sem, self.outer - k, 0)
            for j in range(1, self.inner):
                self.send(
                    slot, slot, self.in_send.at[c, k, j], self.in_recv.at[c, k, j], 0, j
                )
        else:
            staged = self.extra[1].at[k - 1, rows]
            self.add(self.inner_parts(c, k), staged)
            self.send(staged, self.extra[2].at[k - 1, rows], send_sem, recv_sem, k, 0)

    def finish(self, c):
        rows = self.piece(c)
        if self.kind == "gather":
            for k in range(self.outer):
                for j in range(1, self.inner):
                    self.arrived(
                        self.result.at[self.index(self.outer - k, self.inner - j), rows],
                        self.in_send.at[c, k, j],
                        self.in_recv.at[c, k, j],
                        0,
                        self.inner - j,
                    )
        else:
            parts = self.inner_parts(c, 0)
            for k in range(1, self.outer):
                slot = self.extra[2].at[k - 1, rows]
                self.arrived(
                    slot,
                    self.out_send.at[c, k],
                    self.out_recv.at[c, k],
                    self.outer - k,
                    0,
                )
                parts.append(slot)
            self.add(parts, self.result.at[rows])

    def drain(self):
        if self.kind == "gather":
            self.own.wait()
        for copy in self.started:
            copy.wait_send()


def exchange(number, *jobs):
    count = len(jobs)

    def kernel(*refs):
        spare = list(refs[2 * count :])
        for i, job in enumerate(jobs):
            need = len(job.scratch)
            job.bind(refs[i], refs[count + i], spare[:need])
            spare = spare[need:]
        greeted = {job.axis: job for job in jobs}
        barrier = pltpu.get_barrier_semaphore()
        others = [peer for job in greeted.values() for peer in job.peers()]
        for peer in others:
            pl.semaphore_signal(barrier, inc=1, device_id=peer, device_id_type=MESH)
        pl.semaphore_wait(barrier, len(others))
        order = [(c, job) for c in range(max(j.chunks for j in jobs)) for job in jobs]
        order = [(c, job) for c, job in order if c < job.chunks]
        for c, job in order:
            job.start(c)
        for c, job in order:
            for k in range(1, job.outer):
                job.relay(c, k)
        for c, job in order:
            job.finish(c)
        for job in jobs:
            job.drain()

    vmem = pl.BlockSpec(memory_space=pltpu.VMEM)
    return pl.pallas_call(
        kernel,
        out_shape=tuple(job.out for job in jobs),
        in_specs=[vmem] * count,
        out_specs=(vmem,) * count,
        scratch_shapes=[item for job in jobs for item in job.scratch],
        compiler_params=pltpu.CompilerParams(collective_id=number, has_side_effects=True),
        name="exchange" + str(number),
    )(*[job.array for job in jobs])


def dot(form, left, right):
    return jnp.einsum(form, left, right, preferred_element_type=F32)


def per_device(
    tokens, expert_ids, combine_weight, gate_weight, up_weight, down_weight, out_cotangent
):
    groups = lax.axis_size("expert")
    shards = lax.axis_size("tensor")
    local = gate_weight.shape[0]
    width = tokens.shape[1]
    hidden = gate_weight.shape[2]
    rows = tokens.shape[0]
    top = expert_ids.shape[1]
    experts = local * groups
    capacity = 3 * rows * top // (2 * experts)
    slots = groups * capacity
    own = slots // shards
    mine = lax.axis_index("expert")

    named = expert_ids[:, :, None] == jnp.arange(experts, dtype=jnp.int32)
    dense_weight = jnp.sum(jnp.where(named, combine_weight[:, :, None], 0.0), axis=1).T

    def gather(axis, array, chunks=1):
        return Job("gather", axis, lax.axis_size(axis), array, chunks)

    def reduce(axis, array, chunks=1):
        return Job("reduce", axis, lax.axis_size(axis), array, chunks)

    weights_all, tokens_all = exchange(0, gather("expert", dense_weight), gather("expert", tokens, 4))
    weight_tok = lax.dynamic_slice_in_dim(weights_all, mine * local, local, 1)
    weight_tok = weight_tok.transpose(1, 0, 2)
    served = weight_tok > 0.0
    earlier = (jnp.arange(rows)[:, None] < jnp.arange(rows)[None, :]).astype(BF16)
    position = dot("ebs,st->ebt", served.astype(BF16), earlier)
    at_slot = jnp.where(served, position, -1.0).astype(jnp.int32)
    chosen = at_slot[:, :, None, :] == jnp.arange(capacity, dtype=jnp.int32)[:, None]
    place = chosen.astype(BF16)
    weight_slot = jnp.sum(jnp.where(chosen, weight_tok[:, :, None, :], 0.0), axis=3)
    weight_own = lax.dynamic_slice_in_dim(
        weight_slot.reshape(local, slots, 1), lax.axis_index("tensor") * own, own, 1
    )

    def dispatch(values):
        return [
            dot("bct,btd->bcd", place[e], values).astype(BF16).reshape(slots, width)
            for e in range(local)
        ]

    def by_rows(parts):
        return [reduce("tensor", part.reshape(shards, own, hidden), 2) for part in parts]

    def to_rows(parts):
        return [gather("tensor", part.astype(BF16), 2) for part in parts]

    def rows_of(parts):
        return [part.reshape(slots, hidden) for part in parts]

    def each(function, *lists):
        return [function(*[items[e] for items in lists]) for e in range(local)]

    def combine(parts):
        total_sum = sum(
            dot("bct,bcd->btd", place[e], parts[e].reshape(groups, capacity, width))
            for e in range(local)
        )
        return reduce("expert", total_sum.astype(BF16), 4)

    routed = dispatch(tokens_all)
    gate_job = by_rows(
        [dot("cd,dk->ck", routed[e], gate_weight[e]).astype(BF16) for e in range(local)]
    )
    up_job = by_rows(
        [dot("cd,dk->ck", routed[e], up_weight[e]).astype(BF16) for e in range(local)]
    )
    *gate_up, cotangent_all = exchange(
        1, *gate_job, *up_job, gather("expert", out_cotangent, 4)
    )
    gate_up = [part.astype(F32) for part in gate_up]
    gate, up = gate_up[:local], gate_up[local:]
    sigma = each(jax.nn.sigmoid, gate)
    silu = each(lambda g, s: g * s, gate, sigma)
    act = each(lambda a, u: a * u, silu, up)
    incoming = dispatch(cotangent_all)
    pulled_job = by_rows(
        [dot("cd,kd->ck", incoming[e], down_weight[e]).astype(BF16) for e in range(local)]
    )
    pulled_act = exchange(
        2, *pulled_job, *to_rows(each(lambda w, a: w * a, weight_own, act))
    )
    pulled = [part.astype(F32) for part in pulled_act[:local]]
    weighted_act = rows_of(pulled_act[local:])
    weighted_pull = each(lambda w, p: w * p, weight_own, pulled)
    gate_diff = each(
        lambda p, u, s, g: p * u * s * (1.0 + g * (1.0 - s)), weighted_pull, up, sigma, gate
    )
    up_diff = each(lambda p, a: p * a, weighted_pull, silu)
    pair_own = jnp.stack(each(lambda a, p: jnp.sum(a * p, axis=1), act, pulled))
    mixed_job = combine(
        [
            dot("ck,kd->cd", weighted_act[e], down_weight[e]).astype(BF16)
            for e in range(local)
        ]
    )
    mixed, *diffs, pair_all = exchange(
        3, mixed_job, *to_rows(gate_diff), *to_rows(up_diff), gather("tensor", pair_own)
    )
    gate_diff, up_diff = rows_of(diffs[:local]), rows_of(diffs[local:])
    pair_all = pair_all.transpose(1, 0, 2).reshape(local, groups, capacity)
    pair_tok = jnp.sum(jnp.where(chosen, pair_all[:, :, :, None], 0.0), axis=2)
    pair_wide = lax.dynamic_update_slice_in_dim(
        jnp.zeros((groups, experts, rows), F32), pair_tok.transpose(1, 0, 2), mine * local, 1
    )
    token_job = combine(
        [
            (
                dot("ck,dk->cd", gate_diff[e], gate_weight[e])
                + dot("ck,dk->cd", up_diff[e], up_weight[e])
            ).astype(BF16)
            for e in range(local)
        ]
    )
    token_grad, pair_mine = exchange(4, token_job, reduce("expert", pair_wide))
    combine_grad = jnp.sum(jnp.where(named, pair_mine.T[:, None, :], 0.0), axis=2)
    down_grad = jnp.stack(
        [dot("ck,cd->kd", weighted_act[e], incoming[e]).astype(BF16) for e in range(local)]
    )
    gate_grad = jnp.stack(
        [dot("cd,ck->dk", routed[e], gate_diff[e]).astype(BF16) for e in range(local)]
    )
    up_grad = jnp.stack(
        [dot("cd,ck->dk", routed[e], up_diff[e]).astype(BF16) for e in range(local)]
    )
    return (mixed, token_grad, combine_grad, gate_grad, up_grad, down_grad)


def solution(mesh):
    wide, narrow = P("expert", "tensor"), P("expert", None)
    deep, flat = P("expert", "tensor", None), P("expert", None, "tensor")
    return jax.shard_map(
        per_device,
        mesh=mesh,
        in_specs=(wide, narrow, narrow, deep, deep, flat, wide),
        out_specs=(wide, wide, narrow, deep, deep, flat),
        check_vma=False,
    )
```
